32 devices in a mesh: src: 8 (over z, y), tgt: 4 (over x, core).
Axes of the slice: x: 2, y: 2, z: 4, core: 2. Of those that a mesh axis runs over, the one named last changes fastest.
Arguments:
- sources: bfloat16 [8192, 512], P('src'), may hold values from -400 to 400
- log_src: float32 [8192], P('src'), may hold values from -1 to 1
- targets: bfloat16 [2048, 512], P(('src', 'tgt')), may hold values from -6 to 6
- potential: float32 [2048], P(('src', 'tgt')), may hold values from -5 to 5
- log_tgt: float32 [2048], P(('src', 'tgt')), may hold values from -1 to 1
Outputs:
- src_pot: float32 [8192], P('src')
- tgt_pot: float32 [2048], P(('src', 'tgt'))
- mapped: bfloat16 [8192, 512], P('src', 'tgt')
The draws below stay inside these ranges and needn't reach their ends.
All inputs are finite; a program needn't handle non-finite values.
Results may differ from the reference program's by a relative error of at most 0.0144.
Values may be sent and summed in bfloat16 or wider, within the bound.
A program may use at most 64 MiB of HBM per device.

```python
import math
import jax
import jax.numpy as jnp
from jax import lax

F = 512
SRC_DEV = 1024
NS = 8192
NT = 2048
N_SRC = 8


def draw_sources(key, part):
    first = jax.random.fold_in(jax.random.fold_in(key, 17), 0)
    base = jax.random.truncated_normal(first, -6.0, 6.0, (NS, F), jnp.float32)
    return base.astype(jnp.bfloat16)


def block_levels(stream_key, extent, pieces, least, top_value):
    loudness = 1.0
    for dim, parts in pieces:
        steps = jax.random.uniform(jax.random.fold_in(jax.random.fold_in(stream_key, 6), dim), (parts,), jnp.float32, least / len(pieces), top_value / len(pieces))
        loudness = loudness * jnp.repeat(jnp.exp(steps), extent[dim] // parts).reshape((-1,) + (1,) * (len(extent) - 1 - dim))
    return loudness


def centred(own_key, shape, deviation, most, shards=(), held_as=jnp.bfloat16):
    array = deviation * jax.random.normal(own_key, shape, jnp.float32)
    if shards:
        array = array * block_levels(own_key, shape, shards, -0.22, 0.18)
    return jnp.clip(array, -most, most).astype(held_as)


def setup_inputs(seed: int = 0) -> dict:
    key_list = jax.random.split(jax.random.key(seed), 6)
    return {
        "sources": draw_sources(jax.random.fold_in(key_list[5], 71), 0),
        "log_src": jnp.clip(jax.random.uniform(key_list[1], (NS,), jnp.float32, -1.0, 1.0) * block_levels(key_list[1], (NS,), ((0, 8),), -0.4, 0.0), -1.0, 1.0),
        "targets": centred(key_list[2], (NT, F), 1.0, 6.0, ((0, 32),)),
        "potential": centred(key_list[3], (NT,), 1.0, 5.0, ((0, 32),), jnp.float32),
        "log_tgt": jnp.clip(jax.random.uniform(key_list[4], (NT,), jnp.float32, -1.0, 1.0) * block_levels(key_list[4], (NT,), ((0, 32),), -0.4, 0.0), -1.0, 1.0),
    }


def reference(sources, log_src, targets, potential, log_tgt):
    scale = 1.0 / math.sqrt(F)
    points = targets.astype(jnp.float32)
    blocks = sources.astype(jnp.float32).reshape(N_SRC, SRC_DEV, F)
    weights = log_src.reshape(N_SRC, SRC_DEV)

    def scores_of(block):
        return jnp.dot(block, points.T, precision=lax.Precision.HIGHEST) * scale

    def row_pass(items):
        block, logw = items
        shifted = scores_of(block) + potential[None, :]
        top = lax.optimization_barrier(jnp.max(shifted, axis=1))
        total = lax.optimization_barrier(jnp.sum(jnp.exp(shifted - top[:, None]), axis=1))
        return logw - (top + jnp.log(total))
    src_pot = lax.map(row_pass, (blocks, weights))

    def column_pass(items):
        block, pot = items
        lifted = scores_of(block) + pot[:, None]
        top = lax.optimization_barrier(jnp.max(lifted, axis=0))
        return (top, lax.optimization_barrier(jnp.sum(jnp.exp(lifted - top[None, :]), axis=0)))
    tops, totals = lax.map(column_pass, (blocks, src_pot))
    peak = lax.optimization_barrier(jnp.max(tops, axis=0))
    total = lax.optimization_barrier(jnp.sum(totals * jnp.exp(tops - peak[None, :]), axis=0))
    tgt_pot = log_tgt - (peak + jnp.log(total))

    def plan_pass(items):
        block, pot = items
        weight = jnp.exp(scores_of(block) + pot[:, None] + tgt_pot[None, :])
        mass = lax.optimization_barrier(jnp.sum(weight, axis=1))
        plan = weight.astype(jnp.bfloat16).astype(jnp.float32)
        moved = jnp.dot(plan, points, precision=lax.Precision.HIGHEST)
        return (moved / mass[:, None]).astype(jnp.bfloat16)
    mapped = lax.map(plan_pass, (blocks, src_pot)).reshape(NS, F)
    return (src_pot.reshape(NS), tgt_pot, mapped)
```

```python
import functools
import math

import jax
import jax.numpy as jnp
from jax import lax
from jax.experimental import pallas as pl
from jax.experimental.pallas import tpu as pltpu
from jax.sharding import PartitionSpec as P

MESH = pl.DeviceIdType.MESH
LANES = 128


def to_col(row):
    n = row.shape[1]
    eye = lax.broadcasted_iota(jnp.int32, (n, n), 0) == lax.broadcasted_iota(
        jnp.int32, (n, n), 1
    )
    return jnp.sum(jnp.where(eye, row, 0.0), axis=1, keepdims=True)


def to_row(col):
    n = col.shape[0]
    eye = lax.broadcasted_iota(jnp.int32, (n, n), 0) == lax.broadcasted_iota(
        jnp.int32, (n, n), 1
    )
    return jnp.sum(jnp.where(eye, col, 0.0), axis=0, keepdims=True)


def kernel(
    n_src, n_tgt, chunk,
    src_ref, lsrc_ref, tgt_ref, pot_ref, logt_ref,
    spot_ref, tpot_ref, out_ref,
    srcv, src_t, whole, whole_t, scores, q,
    aux, rstat, cstat, mstat, sendp, recvp, keep, sendx, recvx, logt_row, tgt_rows,
    lsem, zs, zr, fs, fr, aus, aur, rs, rr, cs, cr, ms, mr, ps, pr, xs, xr,
):
    s_me, t_me = lax.axis_index("src"), lax.axis_index("tgt")
    a_n, x_n = n_src // 2, n_tgt // 2
    a_me, b_me = s_me // 2, s_me % 2
    x_me, c_me = t_me // 2, t_me % 2
    rows, feats = src_ref.shape
    own = tgt_ref.shape[0]
    group = n_src * own
    half = a_n * own
    width = feats // n_tgt
    pieces = rows // chunk
    scale = 1.0 / math.sqrt(feats)
    slot_me = b_me * a_n + a_me

    def remote(src, dst, send, recv, s, t):
        return pltpu.make_async_remote_copy(
            src_ref=src, dst_ref=dst, send_sem=send, recv_sem=recv,
            device_id=(s, t), device_id_type=MESH,
        )

    load = pltpu.make_async_copy(src_ref, srcv, lsem)
    load.start()

    barrier = pltpu.get_barrier_semaphore()
    for d in range(1, n_src):
        pl.semaphore_signal(
            barrier, inc=1, device_id=((s_me + d) % n_src, t_me), device_id_type=MESH
        )
    for d in range(1, n_tgt):
        pl.semaphore_signal(
            barrier, inc=1, device_id=(s_me, (t_me + d) % n_tgt), device_id_type=MESH
        )
    aux[slot_me] = jnp.zeros(aux.shape[1:], aux.dtype)
    aux[slot_me, 0:1, 0:own] = pot_ref[...]
    aux[slot_me, 1:2, 0:own] = logt_ref[...]
    pl.semaphore_wait(barrier, n_src - 1 + n_tgt - 1)

    def rows_of(slot):
        return whole.at[pl.ds(pl.multiple_of(slot * own, own), own), :]

    sent = []
    order = [d for k in range(1, a_n // 2 + 1) for d in dict.fromkeys((k, a_n - k))]
    copy = remote(tgt_ref, rows_of(slot_me), fs.at[a_me], fr.at[a_me], s_me + 1 - 2 * b_me, t_me)
    copy.start()
    sent.append(copy)
    for d in order:
        a_to = (a_me + d) % a_n
        copy = remote(tgt_ref, rows_of(slot_me), zs.at[a_to], zr.at[a_me], a_to * 2 + b_me, t_me)
        copy.start()
        sent.append(copy)
    for d in range(1, n_src):
        s_to = (s_me + d) % n_src
        copy = remote(aux.at[slot_me], aux.at[slot_me], aus.at[s_to], aur.at[s_me], s_to, t_me)
        copy.start()
        sent.append(copy)
    mine = pltpu.make_async_copy(tgt_ref, rows_of(slot_me), zs.at[a_me])
    mine.start()

    load.wait()
    src_t[...] = srcv[...].T

    for d in range(1, n_src):
        s_from = (s_me + d) % n_src
        slot = (s_from % 2) * a_n + s_from // 2
        remote(aux.at[slot], aux.at[slot], aus.at[s_me], aur.at[s_from], s_from, t_me).wait_recv()

    mine.wait()
    for d in order:
        a_from = (a_me + d) % a_n
        slot = b_me * a_n + a_from
        remote(
            rows_of(slot), rows_of(slot), zs.at[a_me], zr.at[a_from], a_from * 2 + b_me, t_me
        ).wait_recv()
        copy = remote(
            rows_of(slot), rows_of(slot), fs.at[a_from], fr.at[a_from],
            s_me + 1 - 2 * b_me, t_me,
        )
        copy.start()
        sent.append(copy)

    def score_half(b):
        base = pl.multiple_of(b * half, half)
        points = whole[pl.ds(base, half), :]
        pot = jnp.concatenate(
            [to_col(aux[b * a_n + a, 0:1, 0:own]) for a in range(a_n)], axis=0
        )
        stats = []
        for k in range(pieces):
            cols = pl.ds(k * chunk, chunk)
            value = (
                jnp.dot(points, src_t[:, cols], preferred_element_type=jnp.float32) * scale
            )
            scores[pl.ds(base, half), cols] = value
            shifted = value + pot
            top = jnp.max(shifted, axis=0, keepdims=True)
            stats.append((top, jnp.sum(jnp.exp(shifted - top), axis=0, keepdims=True)))
        return stats

    first = score_half(b_me)
    for d in [0] + order:
        a_from = (a_me + d) % a_n
        slot = (1 - b_me) * a_n + a_from
        remote(
            rows_of(slot), rows_of(slot), fs.at[a_from], fr.at[a_from],
            s_me + 1 - 2 * b_me, t_me,
        ).wait_recv()
    second = score_half(1 - b_me)
    for k in range(pieces):
        cols = pl.ds(k * chunk, chunk)
        top = jnp.maximum(first[k][0], second[k][0])
        total = first[k][1] * jnp.exp(first[k][0] - top) + second[k][1] * jnp.exp(
            second[k][0] - top
        )
        rstat[t_me, 0:1, cols] = top
        rstat[t_me, 1:2, cols] = total
    for d in range(1, n_tgt):
        t_to = (t_me + d) % n_tgt
        copy = remote(rstat.at[t_me], rstat.at[t_me], rs.at[t_to], rr.at[t_me], s_me, t_to)
        copy.start()
        sent.append(copy)
    whole_t[...] = whole[...].T
    for slot in range(n_src):
        logt_row[0:1, pl.ds(slot * own, own)] = aux[slot, 1:2, 0:own]
    for d in range(1, n_tgt):
        t_from = (t_me + d) % n_tgt
        remote(
            rstat.at[t_from], rstat.at[t_from], rs.at[t_me], rr.at[t_from], s_me, t_from
        ).wait_recv()
    top = rstat[0, 0:1, :]
    for t in range(1, n_tgt):
        top = jnp.maximum(top, rstat[t, 0:1, :])
    total = rstat[0, 1:2, :] * jnp.exp(rstat[0, 0:1, :] - top)
    for t in range(1, n_tgt):
        total += rstat[t, 1:2, :] * jnp.exp(rstat[t, 0:1, :] - top)
    spot = lsrc_ref[...] - (top + jnp.log(total))
    spot_ref[...] = spot

    for j in range(group // LANES):
        lifted = scores[pl.ds(j * LANES, LANES), :] + spot
        top = jnp.max(lifted, axis=1, keepdims=True)
        e = jnp.exp(lifted - (top - 1.0))
        q[pl.ds(j * LANES, LANES), :] = e.astype(jnp.bfloat16)
        cstat[s_me, 0:1, pl.ds(j * LANES, LANES)] = to_row(top)
        cstat[s_me, 1:2, pl.ds(j * LANES, LANES)] = to_row(
            jnp.sum(e, axis=1, keepdims=True)
        )
    for d in range(1, n_src):
        s_to = (s_me + d) % n_src
        copy = remote(cstat.at[s_me], cstat.at[s_me], cs.at[s_to], cr.at[s_me], s_to, t_me)
        copy.start()
        sent.append(copy)
    for d in range(1, n_src):
        s_from = (s_me + d) % n_src
        remote(
            cstat.at[s_from], cstat.at[s_from], cs.at[s_me], cr.at[s_from], s_from, t_me
        ).wait_recv()
    peak = cstat[0, 0:1, :]
    for s in range(1, n_src):
        peak = jnp.maximum(peak, cstat[s, 0:1, :])
    total = cstat[0, 1:2, :] * jnp.exp(cstat[0, 0:1, :] - peak)
    for s in range(1, n_src):
        total += cstat[s, 1:2, :] * jnp.exp(cstat[s, 0:1, :] - peak)
    tgt_all = logt_row[...] - (peak + (jnp.log(total) - 1.0))
    factor = jnp.exp(cstat[s_me, 0:1, :] + tgt_all - 1.0)
    whole_t[...] = (whole_t[...].astype(jnp.float32) * factor).astype(jnp.bfloat16)

    def block(x, c, k):
        at = pl.multiple_of((x * 2 + c) * width, width)
        return jnp.dot(
            whole_t[pl.ds(at, width), :], q[:, pl.ds(k * chunk, chunk)],
            preferred_element_type=jnp.float32,
        )

    t_pair = x_me * 2 + 1 - c_me

    def to_partner(x, k):
        sendp[x, k] = block(x, 1 - c_me, k).astype(jnp.bfloat16)
        copy = remote(sendp.at[x, k], recvp.at[x, k], ps.at[x, k], pr.at[x, k], s_me, t_pair)
        copy.start()
        sent.append(copy)

    def from_partner(x, k):
        remote(
            sendp.at[x, k], recvp.at[x, k], ps.at[x, k], pr.at[x, k], s_me, t_pair
        ).wait_recv()

    others = [(x_me + d) % x_n for d in range(1, x_n)]
    for x in others:
        for k in range(pieces):
            to_partner(x, k)
    for x in others:
        for k in range(pieces):
            part = block(x, c_me, k)
            from_partner(x, k)
            sendx[x, k] = (part + recvp[x, k].astype(jnp.float32)).astype(jnp.bfloat16)
            copy = remote(
                sendx.at[x, k], recvx.at[x_me, k], xs.at[x, k], xr.at[x_me, k],
                s_me, x * 2 + c_me,
            )
            copy.start()
            sent.append(copy)
    high = factor.astype(jnp.bfloat16)
    low = (factor - high.astype(jnp.float32)).astype(jnp.bfloat16)
    which = lax.broadcasted_iota(jnp.int32, (16, group), 0)
    pair = jnp.where(
        which == 0, high.astype(jnp.float32),
        jnp.where(which == 1, low.astype(jnp.float32), 0.0),
    ).astype(jnp.bfloat16)
    for k in range(pieces):
        cols = pl.ds(k * chunk, chunk)
        both = jnp.dot(pair, q[:, cols], preferred_element_type=jnp.float32)
        mstat[t_me, 0:1, cols] = jnp.sum(both, axis=0, keepdims=True)
    for d in range(1, n_tgt):
        t_to = (t_me + d) % n_tgt
        copy = remote(mstat.at[t_me], mstat.at[t_me], ms.at[t_to], mr.at[t_me], s_me, t_to)
        copy.start()
        sent.append(copy)
    for k in range(pieces):
        to_partner(x_me, k)
    for k in range(pieces):
        keep[k] = block(x_me, c_me, k)
    for slot in range(n_src):
        tgt_rows[slot] = tgt_all[:, slot * own:(slot + 1) * own]
    tpot_ref[...] = tgt_rows[slot_me]
    for d in range(1, n_tgt):
        t_from = (t_me + d) % n_tgt
        remote(
            mstat.at[t_from], mstat.at[t_from], ms.at[t_me], mr.at[t_from], s_me, t_from
        ).wait_recv()
    mass = mstat[0]
    for t in range(1, n_tgt):
        mass += mstat[t]
    for k in range(pieces):
        from_partner(x_me, k)
        keep[k] += recvp[x_me, k].astype(jnp.float32)
    for k in range(pieces):
        value = keep[k]
        for x in others:
            remote(
                sendx.at[x, k], recvx.at[x, k], xs.at[x, k], xr.at[x, k],
                s_me, x * 2 + c_me,
            ).wait_recv()
            value += recvx[x, k].astype(jnp.float32)
        value = value / mass[:, k * chunk:(k + 1) * chunk]
        out_ref[pl.ds(k * chunk, chunk), :] = value.T.astype(jnp.bfloat16)
    for copy in sent:
        copy.wait_send()


def body(n_src, n_tgt, sources, log_src, targets, potential, log_tgt):
    rows, feats = sources.shape
    own = targets.shape[0]
    a_n, x_n = n_src // 2, n_tgt // 2
    group = n_src * own
    width = feats // n_tgt
    chunk = min(256, rows)
    pieces = rows // chunk
    f32, bf16 = jnp.float32, jnp.bfloat16
    dma = pltpu.SemaphoreType.DMA
    vmem = pl.BlockSpec(memory_space=pltpu.VMEM)
    hbm = pl.BlockSpec(memory_space=pl.ANY)
    padded = -(-own // LANES) * LANES
    spot, tpot, mapped = pl.pallas_call(
        functools.partial(kernel, n_src, n_tgt, chunk),
        name="sinkhorn",
        out_shape=(
            jax.ShapeDtypeStruct((1, rows), f32),
            jax.ShapeDtypeStruct((1, own), f32),
            jax.ShapeDtypeStruct((rows, width), bf16),
        ),
        in_specs=[hbm, vmem, hbm, vmem, vmem],
        out_specs=(vmem, vmem, vmem),
        scratch_shapes=[
            pltpu.VMEM((rows, feats), bf16),
            pltpu.VMEM((feats, rows), bf16),
            pltpu.VMEM((group, feats), bf16),
            pltpu.VMEM((feats, group), bf16),
            pltpu.VMEM((group, rows), f32),
            pltpu.VMEM((group, rows), bf16),
            pltpu.VMEM((n_src, 2, padded), f32),
            pltpu.VMEM((n_tgt, 2, rows), f32),
            pltpu.VMEM((n_src, 2, group), f32),
            pltpu.VMEM((n_tgt, 1, rows), f32),
            pltpu.VMEM((x_n, pieces, width, chunk), bf16),
            pltpu.VMEM((x_n, pieces, width, chunk), bf16),
            pltpu.VMEM((pieces, width, chunk), f32),
            pltpu.VMEM((x_n, pieces, width, chunk), bf16),
            pltpu.VMEM((x_n, pieces, width, chunk), bf16),
            pltpu.VMEM((1, group), f32),
            pltpu.VMEM((n_src, 1, own), f32),
            dma,
            dma((a_n,)), dma((a_n,)), dma((a_n,)), dma((a_n,)),
            dma((n_src,)), dma((n_src,)),
            dma((n_tgt,)), dma((n_tgt,)),
            dma((n_src,)), dma((n_src,)),
            dma((n_tgt,)), dma((n_tgt,)),
            dma((x_n, pieces)), dma((x_n, pieces)),
            dma((x_n, pieces)), dma((x_n, pieces)),
        ],
        compiler_params=pltpu.CompilerParams(
            collective_id=0, has_side_effects=True, vmem_limit_bytes=56 * 1024 * 1024
        ),
    )(
        sources, log_src.reshape(1, rows), targets,
        potential.reshape(1, own), log_tgt.reshape(1, own),
    )
    return spot.reshape(rows), tpot.reshape(own), mapped


def solution(mesh):
    placed = (
        P("src", None),
        P("src"),
        P(("src", "tgt"), None),
        P(("src", "tgt")),
        P(("src", "tgt")),
    )
    return jax.shard_map(
        functools.partial(body, mesh.shape["src"], mesh.shape["tgt"]),
        mesh=mesh,
        in_specs=placed,
        out_specs=(P("src"), P(("src", "tgt")), P("src", "tgt")),
        check_vma=False,
    )
```

```python
import functools
import math

import jax
import jax.numpy as jnp
from jax import lax
from jax.experimental import pallas as pl
from jax.experimental.pallas import tpu as pltpu
from jax.sharding import PartitionSpec as P

MESH = pl.DeviceIdType.MESH
LANES = 128


def to_col(row):
    n = row.shape[1]
    eye = lax.broadcasted_iota(jnp.int32, (n, n), 0) == lax.broadcasted_iota(
        jnp.int32, (n, n), 1
    )
    return jnp.sum(jnp.where(eye, row, 0.0), axis=1, keepdims=True)


def to_row(col):
    n = col.shape[0]
    eye = lax.broadcasted_iota(jnp.int32, (n, n), 0) == lax.broadcasted_iota(
        jnp.int32, (n, n), 1
    )
    return jnp.sum(jnp.where(eye, col, 0.0), axis=0, keepdims=True)


def kernel(
    n_src, n_tgt, chunk,
    src_ref, lsrc_hbm, tgt_ref, pot_hbm, logt_hbm,
    spot_ref, tpot_ref, out_ref,
    lsrc_ref, pot_ref, logt_ref, srcv, src_t, whole, whole_t, scores, q,
    aux, rstat, cstat, mstat, sendp, recvp, keep, sendx, recvx, logt_row, tgt_rows,
    lsem, zs, zr, fs, fr, aus, aur, rs, rr, cs, cr, ms, mr, ps, pr, xs, xr,
):
    s_me, t_me = lax.axis_index("src"), lax.axis_index("tgt")
    a_n, x_n = n_src // 2, n_tgt // 2
    a_me, b_me = s_me // 2, s_me % 2
    x_me, c_me = t_me // 2, t_me % 2
    rows, feats = src_ref.shape
    own = tgt_ref.shape[0]
    group = n_src * own
    half = a_n * own
    width = feats // n_tgt
    pieces = rows // chunk
    scale = 1.0 / math.sqrt(feats)
    slot_me = b_me * a_n + a_me

    def remote(src, dst, send, recv, s, t):
        return pltpu.make_async_remote_copy(
            src_ref=src, dst_ref=dst, send_sem=send, recv_sem=recv,
            device_id=(s, t), device_id_type=MESH,
        )

    slot_at = pl.ds(pl.multiple_of(slot_me * own, own), own)
    mine = pltpu.make_async_copy(tgt_ref, whole.at[slot_at, :], zs.at[a_me])
    mine.start()
    small = [
        pltpu.make_async_copy(source, target, lsem.at[1 + i])
        for i, (source, target) in enumerate(
            ((lsrc_hbm, lsrc_ref), (pot_hbm, pot_ref), (logt_hbm, logt_ref))
        )
    ]

    barrier = pltpu.get_barrier_semaphore()
    for d in range(1, n_src):
        pl.semaphore_signal(
            barrier, inc=1, device_id=((s_me + d) % n_src, t_me), device_id_type=MESH
        )
    for d in range(1, n_tgt):
        pl.semaphore_signal(
            barrier, inc=1, device_id=(s_me, (t_me + d) % n_tgt), device_id_type=MESH
        )
    for copy in small:
        copy.start()
    load = pltpu.make_async_copy(src_ref, srcv, lsem.at[0])
    load.start()
    for copy in small:
        copy.wait()
    aux[slot_me] = jnp.zeros(aux.shape[1:], aux.dtype)
    aux[slot_me, 0:1, 0:own] = pot_ref[...]
    aux[slot_me, 1:2, 0:own] = logt_ref[...]
    mine.wait()
    pl.semaphore_wait(barrier, n_src - 1 + n_tgt - 1)

    def rows_of(slot):
        return whole.at[pl.ds(pl.multiple_of(slot * own, own), own), :]

    sent = []
    nearer = jnp.minimum(a_me, a_n - 1 - a_me)
    side = jnp.where(a_me <= a_n - 1 - a_me, 1, -1)

    def nth(k):
        step = (k + 1) // 2 * (side if k % 2 else -side)
        return a_me + jnp.where(k <= 2 * nearer, step, (k - nearer) * side)

    order = list(range(a_n - 1, 0, -1))
    copy = remote(rows_of(slot_me), rows_of(slot_me), fs.at[a_me], fr.at[a_me], s_me + 1 - 2 * b_me, t_me)
    copy.start()
    sent.append(copy)
    for d in order:
        a_to = nth(d)
        copy = remote(rows_of(slot_me), rows_of(slot_me), zs.at[a_to], zr.at[a_me], a_to * 2 + b_me, t_me)
        copy.start()
        sent.append(copy)
    for d in range(1, n_src):
        s_to = (s_me + d) % n_src
        copy = remote(aux.at[slot_me], aux.at[slot_me], aus.at[s_to], aur.at[s_me], s_to, t_me)
        copy.start()
        sent.append(copy)
    load.wait()
    early = rows // 2
    src_t[:, 0:early] = srcv[0:early, :].T

    for d in order:
        a_from = nth(d)
        slot = b_me * a_n + a_from
        remote(
            rows_of(slot), rows_of(slot), zs.at[a_me], zr.at[a_from], a_from * 2 + b_me, t_me
        ).wait_recv()
        copy = remote(
            rows_of(slot), rows_of(slot), fs.at[a_from], fr.at[a_from],
            s_me + 1 - 2 * b_me, t_me,
        )
        copy.start()
        sent.append(copy)

    src_t[:, early:] = srcv[early:, :].T
    for d in range(1, n_src):
        s_from = (s_me + d) % n_src
        slot = (s_from % 2) * a_n + s_from // 2
        remote(aux.at[slot], aux.at[slot], aus.at[s_me], aur.at[s_from], s_from, t_me).wait_recv()

    def score_half(b):
        base = pl.multiple_of(b * half, half)
        points = whole[pl.ds(base, half), :]
        pot = jnp.concatenate(
            [to_col(aux[b * a_n + a, 0:1, 0:own]) for a in range(a_n)], axis=0
        )
        stats = []
        for k in range(pieces):
            cols = pl.ds(k * chunk, chunk)
            value = (
                jnp.dot(points, src_t[:, cols], preferred_element_type=jnp.float32) * scale
            )
            scores[pl.ds(base, half), cols] = value
            shifted = value + pot
            top = jnp.max(shifted, axis=0, keepdims=True)
            stats.append((top, jnp.sum(jnp.exp(shifted - top), axis=0, keepdims=True)))
        return stats

    first = score_half(b_me)
    for d in [0] + order:
        a_from = (a_me + d) % a_n
        slot = (1 - b_me) * a_n + a_from
        remote(
            rows_of(slot), rows_of(slot), fs.at[a_from], fr.at[a_from],
            s_me + 1 - 2 * b_me, t_me,
        ).wait_recv()
    second = score_half(1 - b_me)
    for k in range(pieces):
        cols = pl.ds(k * chunk, chunk)
        top = jnp.maximum(first[k][0], second[k][0])
        total = first[k][1] * jnp.exp(first[k][0] - top) + second[k][1] * jnp.exp(
            second[k][0] - top
        )
        rstat[t_me, 0:1, cols] = top
        rstat[t_me, 1:2, cols] = total
    for d in range(1, n_tgt):
        t_to = (t_me + d) % n_tgt
        copy = remote(rstat.at[t_me], rstat.at[t_me], rs.at[t_to], rr.at[t_me], s_me, t_to)
        copy.start()
        sent.append(copy)
    whole_t[...] = whole[...].T
    for slot in range(n_src):
        logt_row[0:1, pl.ds(slot * own, own)] = aux[slot, 1:2, 0:own]
    for d in range(1, n_tgt):
        t_from = (t_me + d) % n_tgt
        remote(
            rstat.at[t_from], rstat.at[t_from], rs.at[t_me], rr.at[t_from], s_me, t_from
        ).wait_recv()
    top = rstat[0, 0:1, :]
    for t in range(1, n_tgt):
        top = jnp.maximum(top, rstat[t, 0:1, :])
    total = rstat[0, 1:2, :] * jnp.exp(rstat[0, 0:1, :] - top)
    for t in range(1, n_tgt):
        total += rstat[t, 1:2, :] * jnp.exp(rstat[t, 0:1, :] - top)
    spot = lsrc_ref[...] - (top + jnp.log(total))
    spot_ref[...] = spot

    for j in range(group // LANES):
        lifted = scores[pl.ds(j * LANES, LANES), :] + spot
        top = jnp.max(lifted, axis=1, keepdims=True)
        e = jnp.exp(lifted - (top - 1.0))
        q[pl.ds(j * LANES, LANES), :] = e.astype(jnp.bfloat16)
        cstat[s_me, 0:1, pl.ds(j * LANES, LANES)] = to_row(top)
        cstat[s_me, 1:2, pl.ds(j * LANES, LANES)] = to_row(
            jnp.sum(e, axis=1, keepdims=True)
        )
    for d in range(1, n_src):
        s_to = (s_me + d) % n_src
        copy = remote(cstat.at[s_me], cstat.at[s_me], cs.at[s_to], cr.at[s_me], s_to, t_me)
        copy.start()
        sent.append(copy)
    for d in range(1, n_src):
        s_from = (s_me + d) % n_src
        remote(
            cstat.at[s_from], cstat.at[s_from], cs.at[s_me], cr.at[s_from], s_from, t_me
        ).wait_recv()
    peak = cstat[0, 0:1, :]
    for s in range(1, n_src):
        peak = jnp.maximum(peak, cstat[s, 0:1, :])
    total = cstat[0, 1:2, :] * jnp.exp(cstat[0, 0:1, :] - peak)
    for s in range(1, n_src):
        total += cstat[s, 1:2, :] * jnp.exp(cstat[s, 0:1, :] - peak)
    tgt_all = logt_row[...] - (peak + (jnp.log(total) - 1.0))
    factor = jnp.exp(cstat[s_me, 0:1, :] + tgt_all - 1.0)
    whole_t[...] = (whole_t[...].astype(jnp.float32) * factor).astype(jnp.bfloat16)

    def block(x, c, k):
        at = pl.multiple_of((x * 2 + c) * width, width)
        return jnp.dot(
            whole_t[pl.ds(at, width), :], q[:, pl.ds(k * chunk, chunk)],
            preferred_element_type=jnp.float32,
        )

    t_pair = x_me * 2 + 1 - c_me

    def to_partner(x, k):
        sendp[x, k] = block(x, 1 - c_me, k).astype(jnp.bfloat16)
        copy = remote(sendp.at[x, k], recvp.at[x, k], ps.at[x, k], pr.at[x, k], s_me, t_pair)
        copy.start()
        sent.append(copy)

    def from_partner(x, k):
        remote(
            sendp.at[x, k], recvp.at[x, k], ps.at[x, k], pr.at[x, k], s_me, t_pair
        ).wait_recv()

    others = [(x_me + d) % x_n for d in range(1, x_n)]
    for x in others:
        for k in range(pieces):
            to_partner(x, k)
    for x in others:
        for k in range(pieces):
            part = block(x, c_me, k)
            from_partner(x, k)
            sendx[x, k] = (part + recvp[x, k].astype(jnp.float32)).astype(jnp.bfloat16)
            copy = remote(
                sendx.at[x, k], recvx.at[x_me, k], xs.at[x, k], xr.at[x_me, k],
                s_me, x * 2 + c_me,
            )
            copy.start()
            sent.append(copy)
    high = factor.astype(jnp.bfloat16)
    low = (factor - high.astype(jnp.float32)).astype(jnp.bfloat16)
    which = lax.broadcasted_iota(jnp.int32, (16, group), 0)
    pair = jnp.where(
        which == 0, high.astype(jnp.float32),
        jnp.where(which == 1, low.astype(jnp.float32), 0.0),
    ).astype(jnp.bfloat16)
    for k in range(pieces):
        cols = pl.ds(k * chunk, chunk)
        both = jnp.dot(pair, q[:, cols], preferred_element_type=jnp.float32)
        mstat[t_me, 0:1, cols] = jnp.sum(both, axis=0, keepdims=True)
    for d in range(1, n_tgt):
        t_to = (t_me + d) % n_tgt
        copy = remote(mstat.at[t_me], mstat.at[t_me], ms.at[t_to], mr.at[t_me], s_me, t_to)
        copy.start()
        sent.append(copy)
    for k in range(pieces):
        to_partner(x_me, k)
    for k in range(pieces):
        keep[k] = block(x_me, c_me, k)
    for slot in range(n_src):
        tgt_rows[slot] = tgt_all[:, slot * own:(slot + 1) * own]
    tpot_ref[...] = tgt_rows[slot_me]
    for d in range(1, n_tgt):
        t_from = (t_me + d) % n_tgt
        remote(
            mstat.at[t_from], mstat.at[t_from], ms.at[t_me], mr.at[t_from], s_me, t_from
        ).wait_recv()
    mass = mstat[0]
    for t in range(1, n_tgt):
        mass += mstat[t]
    for k in range(pieces):
        from_partner(x_me, k)
        keep[k] += recvp[x_me, k].astype(jnp.float32)
    for k in range(pieces):
        value = keep[k]
        for x in others:
            remote(
                sendx.at[x, k], recvx.at[x, k], xs.at[x, k], xr.at[x, k],
                s_me, x * 2 + c_me,
            ).wait_recv()
            value += recvx[x, k].astype(jnp.float32)
        value = value / mass[:, k * chunk:(k + 1) * chunk]
        out_ref[pl.ds(k * chunk, chunk), :] = value.T.astype(jnp.bfloat16)
    for copy in sent:
        copy.wait_send()


def finish(mapped_ref, spot_ref, tpot_ref, mapped_out, spot_out, tpot_out, sems):
    copies = [
        pltpu.make_async_copy(source, target, sems.at[i])
        for i, (source, target) in enumerate(
            ((mapped_ref, mapped_out), (spot_ref, spot_out), (tpot_ref, tpot_out))
        )
    ]
    for copy in copies:
        copy.start()
    for copy in copies:
        copy.wait()


def body(n_src, n_tgt, sources, log_src, targets, potential, log_tgt):
    rows, feats = sources.shape
    own = targets.shape[0]
    a_n, x_n = n_src // 2, n_tgt // 2
    group = n_src * own
    width = feats // n_tgt
    chunk = min(256, rows)
    pieces = rows // chunk
    f32, bf16 = jnp.float32, jnp.bfloat16
    dma = pltpu.SemaphoreType.DMA
    vmem = pl.BlockSpec(memory_space=pltpu.VMEM)
    hbm = pl.BlockSpec(memory_space=pltpu.HBM)
    padded = -(-own // LANES) * LANES
    spot, tpot, mapped = pl.pallas_call(
        functools.partial(kernel, n_src, n_tgt, chunk),
        name="sinkhorn",
        out_shape=(
            jax.ShapeDtypeStruct((1, rows), f32),
            jax.ShapeDtypeStruct((1, own), f32),
            jax.ShapeDtypeStruct((rows, width), bf16),
        ),
        in_specs=[hbm] * 5,
        out_specs=(vmem, vmem, vmem),
        scratch_shapes=[
            pltpu.VMEM((1, rows), f32),
            pltpu.VMEM((1, own), f32),
            pltpu.VMEM((1, own), f32),
            pltpu.VMEM((rows, feats), bf16),
            pltpu.VMEM((feats, rows), bf16),
            pltpu.VMEM((group, feats), bf16),
            pltpu.VMEM((feats, group), bf16),
            pltpu.VMEM((group, rows), f32),
            pltpu.VMEM((group, rows), bf16),
            pltpu.VMEM((n_src, 2, padded), f32),
            pltpu.VMEM((n_tgt, 2, rows), f32),
            pltpu.VMEM((n_src, 2, group), f32),
            pltpu.VMEM((n_tgt, 1, rows), f32),
            pltpu.VMEM((x_n, pieces, width, chunk), bf16),
            pltpu.VMEM((x_n, pieces, width, chunk), bf16),
            pltpu.VMEM((pieces, width, chunk), f32),
            pltpu.VMEM((x_n, pieces, width, chunk), bf16),
            pltpu.VMEM((x_n, pieces, width, chunk), bf16),
            pltpu.VMEM((1, group), f32),
            pltpu.VMEM((n_src, 1, own), f32),
            dma((4,)),
            dma((a_n,)), dma((a_n,)), dma((a_n,)), dma((a_n,)),
            dma((n_src,)), dma((n_src,)),
            dma((n_tgt,)), dma((n_tgt,)),
            dma((n_src,)), dma((n_src,)),
            dma((n_tgt,)), dma((n_tgt,)),
            dma((x_n, pieces)), dma((x_n, pieces)),
            dma((x_n, pieces)), dma((x_n, pieces)),
        ],
        compiler_params=pltpu.CompilerParams(
            collective_id=0, has_side_effects=True, vmem_limit_bytes=40 * 1024 * 1024
        ),
    )(
        *(
            pltpu.with_memory_space_constraint(array, pltpu.HBM)
            for array in (
                sources, log_src.reshape(1, rows), targets,
                potential.reshape(1, own), log_tgt.reshape(1, own),
            )
        )
    )
    mapped, spot, tpot = pl.pallas_call(
        finish,
        name="finish",
        out_shape=(
            jax.ShapeDtypeStruct((rows, width), bf16),
            jax.ShapeDtypeStruct((1, rows), f32),
            jax.ShapeDtypeStruct((1, own), f32),
        ),
        in_specs=[pl.BlockSpec(memory_space=pl.ANY)] * 3,
        out_specs=(hbm,) * 3,
        scratch_shapes=[dma((3,))],
        compiler_params=pltpu.CompilerParams(vmem_limit_bytes=1024 * 1024),
    )(mapped, spot, tpot)
    return spot.reshape(rows), tpot.reshape(own), mapped


def solution(mesh):
    placed = (
        P("src", None),
        P("src"),
        P(("src", "tgt"), None),
        P(("src", "tgt")),
        P(("src", "tgt")),
    )
    return jax.shard_map(
        functools.partial(body, mesh.shape["src"], mesh.shape["tgt"]),
        mesh=mesh,
        in_specs=placed,
        out_specs=(P("src"), P(("src", "tgt")), P("src", "tgt")),
        check_vma=False,
    )
```

```python
import functools
import math

import jax
import jax.numpy as jnp
from jax import lax
from jax.experimental import pallas as pl
from jax.experimental.pallas import tpu as pltpu
from jax.sharding import PartitionSpec as P

MESH = pl.DeviceIdType.MESH
LANES = 128


def to_col(row):
    n = row.shape[1]
    eye = lax.broadcasted_iota(jnp.int32, (n, n), 0) == lax.broadcasted_iota(
        jnp.int32, (n, n), 1
    )
    return jnp.sum(jnp.where(eye, row, 0.0), axis=1, keepdims=True)


def to_row(col):
    n = col.shape[0]
    eye = lax.broadcasted_iota(jnp.int32, (n, n), 0) == lax.broadcasted_iota(
        jnp.int32, (n, n), 1
    )
    return jnp.sum(jnp.where(eye, col, 0.0), axis=0, keepdims=True)


def joined(parts):
    top = functools.reduce(jnp.maximum, parts)
    return top + jnp.log(sum(jnp.exp(part - top) for part in parts))


def kernel(
    n_src, n_tgt, chunk,
    src_ref, lsrc_hbm, tgt_ref, pot_hbm, logt_hbm,
    spot_ref, tpot_ref, out_ref,
    lsrc_ref, pot_ref, logt_ref, srcv, src_t, whole, whole_t, scores, q,
    aux, rstat, cstat, mstat, sendp, recvp, keep, sendx, recvx, logt_row, tops, tgt_rows,
    lsem, zs, zr, fs, fr, aus, aur, rs, rr, cs, cr, ms, mr, ps, pr, xs, xr,
):
    s_me, t_me = lax.axis_index("src"), lax.axis_index("tgt")
    a_n, x_n = n_src // 2, n_tgt // 2
    a_me, b_me = s_me // 2, s_me % 2
    x_me, c_me = t_me // 2, t_me % 2
    rows, feats = src_ref.shape
    own = tgt_ref.shape[0]
    group = n_src * own
    half = a_n * own
    width = feats // n_tgt
    pieces = rows // chunk
    scale = 1.0 / math.sqrt(feats)
    slot_me = b_me * a_n + a_me

    def remote(src, dst, send, recv, s, t):
        return pltpu.make_async_remote_copy(
            src_ref=src, dst_ref=dst, send_sem=send, recv_sem=recv,
            device_id=(s, t), device_id_type=MESH,
        )

    slot_at = pl.ds(pl.multiple_of(slot_me * own, own), own)
    mine = pltpu.make_async_copy(tgt_ref, whole.at[slot_at, :], zs.at[a_me])
    mine.start()
    small = [
        pltpu.make_async_copy(source, target, lsem.at[1 + i])
        for i, (source, target) in enumerate(
            ((lsrc_hbm, lsrc_ref), (pot_hbm, pot_ref), (logt_hbm, logt_ref))
        )
    ]

    barrier = pltpu.get_barrier_semaphore()
    for d in range(1, n_src):
        pl.semaphore_signal(
            barrier, inc=1, device_id=((s_me + d) % n_src, t_me), device_id_type=MESH
        )
    for d in range(1, n_tgt):
        pl.semaphore_signal(
            barrier, inc=1, device_id=(s_me, (t_me + d) % n_tgt), device_id_type=MESH
        )
    for copy in small:
        copy.start()
    load = pltpu.make_async_copy(src_ref, srcv, lsem.at[0])
    load.start()
    for copy in small:
        copy.wait()
    aux[slot_me] = jnp.zeros(aux.shape[1:], aux.dtype)
    aux[slot_me, 0:1, 0:own] = pot_ref[...]
    aux[slot_me, 1:2, 0:own] = logt_ref[...]
    mine.wait()
    pl.semaphore_wait(barrier, n_src - 1 + n_tgt - 1)

    def rows_of(slot):
        return whole.at[pl.ds(pl.multiple_of(slot * own, own), own), :]

    sent = []
    nearer = jnp.minimum(a_me, a_n - 1 - a_me)
    side = jnp.where(a_me <= a_n - 1 - a_me, 1, -1)

    def nth(k):
        step = (k + 1) // 2 * (side if k % 2 else -side)
        return a_me + jnp.where(k <= 2 * nearer, step, (k - nearer) * side)

    order = list(range(a_n - 1, 0, -1))
    copy = remote(rows_of(slot_me), rows_of(slot_me), fs.at[a_me], fr.at[a_me], s_me + 1 - 2 * b_me, t_me)
    copy.start()
    sent.append(copy)
    for d in order:
        a_to = nth(d)
        copy = remote(rows_of(slot_me), rows_of(slot_me), zs.at[a_to], zr.at[a_me], a_to * 2 + b_me, t_me)
        copy.start()
        sent.append(copy)
    for d in range(1, n_src):
        s_to = (s_me + d) % n_src
        copy = remote(aux.at[slot_me], aux.at[slot_me], aus.at[s_to], aur.at[s_me], s_to, t_me)
        copy.start()
        sent.append(copy)
    load.wait()
    for d in order:
        a_from = nth(d)
        slot = b_me * a_n + a_from
        remote(
            rows_of(slot), rows_of(slot), zs.at[a_me], zr.at[a_from], a_from * 2 + b_me, t_me
        ).wait_recv()
        copy = remote(
            rows_of(slot), rows_of(slot), fs.at[a_from], fr.at[a_from],
            s_me + 1 - 2 * b_me, t_me,
        )
        copy.start()
        sent.append(copy)

    src_t[...] = srcv[...].T
    for d in range(1, n_src):
        s_from = (s_me + d) % n_src
        slot = (s_from % 2) * a_n + s_from // 2
        remote(aux.at[slot], aux.at[slot], aus.at[s_me], aur.at[s_from], s_from, t_me).wait_recv()

    def score_half(b):
        base = pl.multiple_of(b * half, half)
        points = whole[pl.ds(base, half), :]
        pot = jnp.concatenate(
            [to_col(aux[b * a_n + a, 0:1, 0:own]) for a in range(a_n)], axis=0
        )
        stats = []
        for k in range(pieces):
            cols = pl.ds(k * chunk, chunk)
            value = (
                jnp.dot(points, src_t[:, cols], preferred_element_type=jnp.float32) * scale
            )
            scores[pl.ds(base, half), cols] = value
            shifted = value + pot
            top = jnp.max(shifted, axis=0, keepdims=True)
            stats.append((top, jnp.sum(jnp.exp(shifted - top), axis=0, keepdims=True)))
        return stats

    first = score_half(b_me)
    for d in [0] + order:
        a_from = (a_me + d) % a_n
        slot = (1 - b_me) * a_n + a_from
        remote(
            rows_of(slot), rows_of(slot), fs.at[a_from], fr.at[a_from],
            s_me + 1 - 2 * b_me, t_me,
        ).wait_recv()
    second = score_half(1 - b_me)
    for k in range(pieces):
        cols = pl.ds(k * chunk, chunk)
        top = jnp.maximum(first[k][0], second[k][0])
        total = first[k][1] * jnp.exp(first[k][0] - top) + second[k][1] * jnp.exp(
            second[k][0] - top
        )
        rstat[t_me, 0:1, cols] = top + jnp.log(total)
    for d in [n_tgt // 2] + [d for d in range(1, n_tgt) if d != n_tgt // 2]:
        t_to = (t_me + d) % n_tgt
        copy = remote(rstat.at[t_me], rstat.at[t_me], rs.at[t_to], rr.at[t_me], s_me, t_to)
        copy.start()
        sent.append(copy)
    whole_t[...] = whole[...].T
    for slot in range(n_src):
        logt_row[0:1, pl.ds(slot * own, own)] = aux[slot, 1:2, 0:own]
    for d in range(1, n_tgt):
        t_from = (t_me + d) % n_tgt
        remote(
            rstat.at[t_from], rstat.at[t_from], rs.at[t_me], rr.at[t_from], s_me, t_from
        ).wait_recv()
    spot = lsrc_ref[...] - joined([rstat[t] for t in range(n_tgt)])
    spot_ref[...] = spot

    for j in range(group // LANES):
        lifted = scores[pl.ds(j * LANES, LANES), :] + spot
        top = jnp.max(lifted, axis=1, keepdims=True)
        e = jnp.exp(lifted - (top - 1.0))
        q[pl.ds(j * LANES, LANES), :] = e.astype(jnp.bfloat16)
        top, total = to_row(top), to_row(jnp.sum(e, axis=1, keepdims=True))
        tops[0:1, pl.ds(j * LANES, LANES)] = top
        cstat[s_me, 0:1, pl.ds(j * LANES, LANES)] = top + (jnp.log(total) - 1.0)
    for a_to, flip in [(nth(k) if k else None, f) for k in order + [0] for f in (1, 0) if k or f]:
        s_to = (a_me if a_to is None else a_to) * 2 + (1 - b_me if flip else b_me)
        copy = remote(cstat.at[s_me], cstat.at[s_me], cs.at[s_to], cr.at[s_me], s_to, t_me)
        copy.start()
        sent.append(copy)
    for d in range(1, n_src):
        s_from = (s_me + d) % n_src
        remote(
            cstat.at[s_from], cstat.at[s_from], cs.at[s_me], cr.at[s_from], s_from, t_me
        ).wait_recv()
    tgt_all = logt_row[...] - joined([cstat[s] for s in range(n_src)])
    factor = jnp.exp(tops[...] + tgt_all - 1.0)
    whole_t[...] = (whole_t[...].astype(jnp.float32) * factor).astype(jnp.bfloat16)

    def block(x, c, k):
        at = pl.multiple_of((x * 2 + c) * width, width)
        return jnp.dot(
            whole_t[pl.ds(at, width), :], q[:, pl.ds(k * chunk, chunk)],
            preferred_element_type=jnp.float32,
        )

    t_pair = x_me * 2 + 1 - c_me

    def to_partner(x, k):
        sendp[x, k] = block(x, 1 - c_me, k).astype(jnp.bfloat16)
        copy = remote(sendp.at[x, k], recvp.at[x, k], ps.at[x, k], pr.at[x, k], s_me, t_pair)
        copy.start()
        sent.append(copy)

    def from_partner(x, k):
        remote(
            sendp.at[x, k], recvp.at[x, k], ps.at[x, k], pr.at[x, k], s_me, t_pair
        ).wait_recv()

    others = [(x_me + d) % x_n for d in range(1, x_n)]
    for x in others:
        to_partner(x, 0)
    for x in others:
        for k in range(pieces):
            if k + 1 < pieces:
                to_partner(x, k + 1)
            part = block(x, c_me, k)
            from_partner(x, k)
            sendx[x, k] = (part + recvp[x, k].astype(jnp.float32)).astype(jnp.bfloat16)
            copy = remote(
                sendx.at[x, k], recvx.at[x_me, k], xs.at[x, k], xr.at[x_me, k],
                s_me, x * 2 + c_me,
            )
            copy.start()
            sent.append(copy)
    high = factor.astype(jnp.bfloat16)
    low = (factor - high.astype(jnp.float32)).astype(jnp.bfloat16)
    which = lax.broadcasted_iota(jnp.int32, (16, group), 0)
    pair = jnp.where(
        which == 0, high.astype(jnp.float32),
        jnp.where(which == 1, low.astype(jnp.float32), 0.0),
    ).astype(jnp.bfloat16)
    for k in range(pieces):
        cols = pl.ds(k * chunk, chunk)
        both = jnp.dot(pair, q[:, cols], preferred_element_type=jnp.float32)
        mstat[t_me, 0:1, cols] = jnp.sum(both, axis=0, keepdims=True)
    for d in range(1, n_tgt):
        t_to = (t_me + d) % n_tgt
        copy = remote(mstat.at[t_me], mstat.at[t_me], ms.at[t_to], mr.at[t_me], s_me, t_to)
        copy.start()
        sent.append(copy)
    for k in range(pieces):
        to_partner(x_me, k)
    for k in range(pieces):
        keep[k] = block(x_me, c_me, k)
    for slot in range(n_src):
        tgt_rows[slot] = tgt_all[:, slot * own:(slot + 1) * own]
    tpot_ref[...] = tgt_rows[slot_me]
    for d in range(1, n_tgt):
        t_from = (t_me + d) % n_tgt
        remote(
            mstat.at[t_from], mstat.at[t_from], ms.at[t_me], mr.at[t_from], s_me, t_from
        ).wait_recv()
    mass = mstat[0]
    for t in range(1, n_tgt):
        mass += mstat[t]
    for k in range(pieces):
        from_partner(x_me, k)
        keep[k] += recvp[x_me, k].astype(jnp.float32)
    for k in range(pieces):
        value = keep[k]
        for x in others:
            remote(
                sendx.at[x, k], recvx.at[x, k], xs.at[x, k], xr.at[x, k],
                s_me, x * 2 + c_me,
            ).wait_recv()
            value += recvx[x, k].astype(jnp.float32)
        value = value / mass[:, k * chunk:(k + 1) * chunk]
        out_ref[pl.ds(k * chunk, chunk), :] = value.T.astype(jnp.bfloat16)
    for copy in sent:
        copy.wait_send()


def finish(mapped_ref, spot_ref, tpot_ref, mapped_out, spot_out, tpot_out, sems):
    copies = [
        pltpu.make_async_copy(source, target, sems.at[i])
        for i, (source, target) in enumerate(
            ((mapped_ref, mapped_out), (spot_ref, spot_out), (tpot_ref, tpot_out))
        )
    ]
    for copy in copies:
        copy.start()
    for copy in copies:
        copy.wait()


def body(n_src, n_tgt, sources, log_src, targets, potential, log_tgt):
    rows, feats = sources.shape
    own = targets.shape[0]
    a_n, x_n = n_src // 2, n_tgt // 2
    group = n_src * own
    width = feats // n_tgt
    chunk = min(512, rows)
    pieces = rows // chunk
    f32, bf16 = jnp.float32, jnp.bfloat16
    dma = pltpu.SemaphoreType.DMA
    vmem = pl.BlockSpec(memory_space=pltpu.VMEM)
    hbm = pl.BlockSpec(memory_space=pltpu.HBM)
    padded = -(-own // LANES) * LANES
    spot, tpot, mapped = pl.pallas_call(
        functools.partial(kernel, n_src, n_tgt, chunk),
        name="sinkhorn",
        out_shape=(
            jax.ShapeDtypeStruct((1, rows), f32),
            jax.ShapeDtypeStruct((1, own), f32),
            jax.ShapeDtypeStruct((rows, width), bf16),
        ),
        in_specs=[hbm] * 5,
        out_specs=(vmem, vmem, vmem),
        scratch_shapes=[
            pltpu.VMEM((1, rows), f32),
            pltpu.VMEM((1, own), f32),
            pltpu.VMEM((1, own), f32),
            pltpu.VMEM((rows, feats), bf16),
            pltpu.VMEM((feats, rows), bf16),
            pltpu.VMEM((group, feats), bf16),
            pltpu.VMEM((feats, group), bf16),
            pltpu.VMEM((group, rows), f32),
            pltpu.VMEM((group, rows), bf16),
            pltpu.VMEM((n_src, 2, padded), f32),
            pltpu.VMEM((n_tgt, 1, rows), f32),
            pltpu.VMEM((n_src, 1, group), f32),
            pltpu.VMEM((n_tgt, 1, rows), f32),
            pltpu.VMEM((x_n, pieces, width, chunk), bf16),
            pltpu.VMEM((x_n, pieces, width, chunk), bf16),
            pltpu.VMEM((pieces, width, chunk), f32),
            pltpu.VMEM((x_n, pieces, width, chunk), bf16),
            pltpu.VMEM((x_n, pieces, width, chunk), bf16),
            pltpu.VMEM((1, group), f32),
            pltpu.VMEM((1, group), f32),
            pltpu.VMEM((n_src, 1, own), f32),
            dma((4,)),
            dma((a_n,)), dma((a_n,)), dma((a_n,)), dma((a_n,)),
            dma((n_src,)), dma((n_src,)),
            dma((n_tgt,)), dma((n_tgt,)),
            dma((n_src,)), dma((n_src,)),
            dma((n_tgt,)), dma((n_tgt,)),
            dma((x_n, pieces)), dma((x_n, pieces)),
            dma((x_n, pieces)), dma((x_n, pieces)),
        ],
        compiler_params=pltpu.CompilerParams(
            collective_id=0, has_side_effects=True, vmem_limit_bytes=40 * 1024 * 1024
        ),
    )(
        *(
            pltpu.with_memory_space_constraint(array, pltpu.HBM)
            for array in (
                sources, log_src.reshape(1, rows), targets,
                potential.reshape(1, own), log_tgt.reshape(1, own),
            )
        )
    )
    mapped, spot, tpot = pl.pallas_call(
        finish,
        name="finish",
        out_shape=(
            jax.ShapeDtypeStruct((rows, width), bf16),
            jax.ShapeDtypeStruct((1, rows), f32),
            jax.ShapeDtypeStruct((1, own), f32),
        ),
        in_specs=[pl.BlockSpec(memory_space=pl.ANY)] * 3,
        out_specs=(hbm,) * 3,
        scratch_shapes=[dma((3,))],
        compiler_params=pltpu.CompilerParams(vmem_limit_bytes=1024 * 1024),
    )(mapped, spot, tpot)
    return spot.reshape(rows), tpot.reshape(own), mapped


def solution(mesh):
    placed = (
        P("src", None),
        P("src"),
        P(("src", "tgt"), None),
        P(("src", "tgt")),
        P(("src", "tgt")),
    )
    return jax.shard_map(
        functools.partial(body, mesh.shape["src"], mesh.shape["tgt"]),
        mesh=mesh,
        in_specs=placed,
        out_specs=(P("src"), P(("src", "tgt")), P("src", "tgt")),
        check_vma=False,
    )
```

```python
import functools
import math

import jax
import jax.numpy as jnp
from jax import lax
from jax.experimental import pallas as pl
from jax.experimental.pallas import tpu as pltpu
from jax.sharding import PartitionSpec as P

MESH = pl.DeviceIdType.MESH
LANES = 128


def to_col(row):
    n = row.shape[1]
    eye = lax.broadcasted_iota(jnp.int32, (n, n), 0) == lax.broadcasted_iota(
        jnp.int32, (n, n), 1
    )
    return jnp.sum(jnp.where(eye, row, 0.0), axis=1, keepdims=True)


def to_row(col):
    n = col.shape[0]
    eye = lax.broadcasted_iota(jnp.int32, (n, n), 0) == lax.broadcasted_iota(
        jnp.int32, (n, n), 1
    )
    return jnp.sum(jnp.where(eye, col, 0.0), axis=0, keepdims=True)


def joined(parts):
    top = functools.reduce(jnp.maximum, parts)
    return top + jnp.log(sum(jnp.exp(part - top) for part in parts))


def kernel(
    n_src, n_tgt, chunk,
    src_ref, lsrc_hbm, tgt_ref, pot_hbm, logt_hbm,
    spot_ref, tpot_ref, out_ref,
    lsrc_ref, pot_ref, logt_ref, srcv, src_t, whole, whole_t, scores, q,
    aux, rstat, cstat, mstat, sendp, recvp, keep, sendx, recvx, logt_row, tops, tgt_rows,
    lsem, zs, zr, fs, fr, aus, aur, rs, rr, cs, cr, ms, mr, ps, pr, xs, xr,
):
    s_me, t_me = lax.axis_index("src"), lax.axis_index("tgt")
    a_n, x_n = n_src // 2, n_tgt // 2
    a_me, b_me = s_me // 2, s_me % 2
    x_me, c_me = t_me // 2, t_me % 2
    rows, feats = src_ref.shape
    own = tgt_ref.shape[0]
    group = n_src * own
    half = a_n * own
    width = feats // n_tgt
    pieces = rows // chunk
    scale = 1.0 / math.sqrt(feats)
    slot_me = b_me * a_n + a_me

    def remote(src, dst, send, recv, s, t):
        return pltpu.make_async_remote_copy(
            src_ref=src, dst_ref=dst, send_sem=send, recv_sem=recv,
            device_id=(s, t), device_id_type=MESH,
        )

    slot_at = pl.ds(pl.multiple_of(slot_me * own, own), own)
    mine = pltpu.make_async_copy(tgt_ref, whole.at[slot_at, :], zs.at[a_me])
    mine.start()
    small = [
        pltpu.make_async_copy(source, target, lsem.at[1 + i])
        for i, (source, target) in enumerate(
            ((lsrc_hbm, lsrc_ref), (pot_hbm, pot_ref), (logt_hbm, logt_ref))
        )
    ]

    barrier = pltpu.get_barrier_semaphore()
    for d in range(1, n_src):
        pl.semaphore_signal(
            barrier, inc=1, device_id=((s_me + d) % n_src, t_me), device_id_type=MESH
        )
    for d in range(1, n_tgt):
        pl.semaphore_signal(
            barrier, inc=1, device_id=(s_me, (t_me + d) % n_tgt), device_id_type=MESH
        )
    for copy in small:
        copy.start()
    load = pltpu.make_async_copy(src_ref, srcv, lsem.at[0])
    load.start()
    for copy in small:
        copy.wait()
    aux[slot_me] = jnp.zeros(aux.shape[1:], aux.dtype)
    aux[slot_me, 0:1, 0:own] = pot_ref[...]
    aux[slot_me, 1:2, 0:own] = logt_ref[...]
    mine.wait()
    pl.semaphore_wait(barrier, n_src - 1 + n_tgt - 1)

    def rows_of(slot):
        return whole.at[pl.ds(pl.multiple_of(slot * own, own), own), :]

    sent = []
    nearer = jnp.minimum(a_me, a_n - 1 - a_me)
    side = jnp.where(a_me <= a_n - 1 - a_me, 1, -1)

    def nth(k):
        step = (k + 1) // 2 * (side if k % 2 else -side)
        return a_me + jnp.where(k <= 2 * nearer, step, (k - nearer) * side)

    order = list(range(a_n - 1, 0, -1))
    copy = remote(rows_of(slot_me), rows_of(slot_me), fs.at[a_me], fr.at[a_me], s_me + 1 - 2 * b_me, t_me)
    copy.start()
    sent.append(copy)
    for d in order:
        a_to = nth(d)
        copy = remote(rows_of(slot_me), rows_of(slot_me), zs.at[a_to], zr.at[a_me], a_to * 2 + b_me, t_me)
        copy.start()
        sent.append(copy)
    for d in range(1, n_src):
        s_to = (s_me + d) % n_src
        copy = remote(aux.at[slot_me], aux.at[slot_me], aus.at[s_to], aur.at[s_me], s_to, t_me)
        copy.start()
        sent.append(copy)
    load.wait()
    for d in order:
        a_from = nth(d)
        slot = b_me * a_n + a_from
        remote(
            rows_of(slot), rows_of(slot), zs.at[a_me], zr.at[a_from], a_from * 2 + b_me, t_me
        ).wait_recv()
        copy = remote(
            rows_of(slot), rows_of(slot), fs.at[a_from], fr.at[a_from],
            s_me + 1 - 2 * b_me, t_me,
        )
        copy.start()
        sent.append(copy)

    src_t[...] = srcv[...].T
    for d in range(1, n_src):
        s_from = (s_me + d) % n_src
        slot = (s_from % 2) * a_n + s_from // 2
        remote(aux.at[slot], aux.at[slot], aus.at[s_me], aur.at[s_from], s_from, t_me).wait_recv()

    def score_half(b):
        base = pl.multiple_of(b * half, half)
        points = whole[pl.ds(base, half), :]
        pot = jnp.concatenate(
            [to_col(aux[b * a_n + a, 0:1, 0:own]) for a in range(a_n)], axis=0
        )
        stats = []
        for k in range(pieces):
            cols = pl.ds(k * chunk, chunk)
            value = (
                jnp.dot(points, src_t[:, cols], preferred_element_type=jnp.float32) * scale
            )
            scores[pl.ds(base, half), cols] = value
            shifted = value + pot
            top = jnp.max(shifted, axis=0, keepdims=True)
            stats.append((top, jnp.sum(jnp.exp(shifted - top), axis=0, keepdims=True)))
        return stats

    first = score_half(b_me)
    for d in [0] + order:
        a_from = (a_me + d) % a_n
        slot = (1 - b_me) * a_n + a_from
        remote(
            rows_of(slot), rows_of(slot), fs.at[a_from], fr.at[a_from],
            s_me + 1 - 2 * b_me, t_me,
        ).wait_recv()
    second = score_half(1 - b_me)
    for k in range(pieces):
        cols = pl.ds(k * chunk, chunk)
        top = jnp.maximum(first[k][0], second[k][0])
        total = first[k][1] * jnp.exp(first[k][0] - top) + second[k][1] * jnp.exp(
            second[k][0] - top
        )
        rstat[t_me, 0:1, cols] = top + jnp.log(total)
    for d in [n_tgt // 2] + [d for d in range(1, n_tgt) if d != n_tgt // 2]:
        t_to = (t_me + d) % n_tgt
        copy = remote(rstat.at[t_me], rstat.at[t_me], rs.at[t_to], rr.at[t_me], s_me, t_to)
        copy.start()
        sent.append(copy)
    whole_t[...] = whole[...].T
    for slot in range(n_src):
        logt_row[0:1, pl.ds(slot * own, own)] = aux[slot, 1:2, 0:own]
    for d in range(1, n_tgt):
        t_from = (t_me + d) % n_tgt
        remote(
            rstat.at[t_from], rstat.at[t_from], rs.at[t_me], rr.at[t_from], s_me, t_from
        ).wait_recv()
    spot = lsrc_ref[...] - joined([rstat[t] for t in range(n_tgt)])
    spot_ref[...] = spot

    for j in range(group // LANES):
        lifted = scores[pl.ds(j * LANES, LANES), :] + spot
        top = jnp.max(lifted, axis=1, keepdims=True)
        e = jnp.exp(lifted - (top - 1.0))
        q[pl.ds(j * LANES, LANES), :] = e.astype(jnp.bfloat16)
        top, total = to_row(top), to_row(jnp.sum(e, axis=1, keepdims=True))
        tops[0:1, pl.ds(j * LANES, LANES)] = top
        cstat[s_me, 0:1, pl.ds(j * LANES, LANES)] = top + (jnp.log(total) - 1.0)
    for a_to, flip in [(nth(k) if k else None, f) for k in order + [0] for f in (1, 0) if k or f]:
        s_to = (a_me if a_to is None else a_to) * 2 + (1 - b_me if flip else b_me)
        copy = remote(cstat.at[s_me], cstat.at[s_me], cs.at[s_to], cr.at[s_me], s_to, t_me)
        copy.start()
        sent.append(copy)
    for d in range(1, n_src):
        s_from = (s_me + d) % n_src
        remote(
            cstat.at[s_from], cstat.at[s_from], cs.at[s_me], cr.at[s_from], s_from, t_me
        ).wait_recv()
    tgt_all = logt_row[...] - joined([cstat[s] for s in range(n_src)])
    factor = jnp.exp(tops[...] + tgt_all - 1.0)

    def block(x, c, k):
        at = pl.multiple_of((x * 2 + c) * width, width)
        points = (whole_t[pl.ds(at, width), :].astype(jnp.float32) * factor).astype(jnp.bfloat16)
        return jnp.dot(
            points, q[:, pl.ds(k * chunk, chunk)],
            preferred_element_type=jnp.float32,
        )

    t_pair = x_me * 2 + 1 - c_me

    def to_partner(x, k):
        sendp[x, k] = block(x, 1 - c_me, k).astype(jnp.bfloat16)
        copy = remote(sendp.at[x, k], recvp.at[x, k], ps.at[x, k], pr.at[x, k], s_me, t_pair)
        copy.start()
        sent.append(copy)

    def from_partner(x, k):
        remote(
            sendp.at[x, k], recvp.at[x, k], ps.at[x, k], pr.at[x, k], s_me, t_pair
        ).wait_recv()

    others = [(x_me + d) % x_n for d in range(1, x_n)]
    for x in others:
        to_partner(x, 0)
    high = factor.astype(jnp.bfloat16)
    low = (factor - high.astype(jnp.float32)).astype(jnp.bfloat16)
    which = lax.broadcasted_iota(jnp.int32, (16, group), 0)
    pair = jnp.where(
        which == 0, high.astype(jnp.float32),
        jnp.where(which == 1, low.astype(jnp.float32), 0.0),
    ).astype(jnp.bfloat16)
    for k in range(pieces):
        cols = pl.ds(k * chunk, chunk)
        both = jnp.dot(pair, q[:, cols], preferred_element_type=jnp.float32)
        mstat[t_me, 0:1, cols] = jnp.sum(both, axis=0, keepdims=True)
    for d in range(1, n_tgt):
        t_to = (t_me + d) % n_tgt
        copy = remote(mstat.at[t_me], mstat.at[t_me], ms.at[t_to], mr.at[t_me], s_me, t_to)
        copy.start()
        sent.append(copy)
    for x in others:
        for k in range(pieces):
            if k + 1 < pieces:
                to_partner(x, k + 1)
            part = block(x, c_me, k)
            from_partner(x, k)
            sendx[x, k] = (part + recvp[x, k].astype(jnp.float32)).astype(jnp.bfloat16)
            copy = remote(
                sendx.at[x, k], recvx.at[x_me, k], xs.at[x, k], xr.at[x_me, k],
                s_me, x * 2 + c_me,
            )
            copy.start()
            sent.append(copy)
    for k in range(pieces):
        to_partner(x_me, k)
    for k in range(pieces):
        keep[k] = block(x_me, c_me, k)
    for slot in range(n_src):
        tgt_rows[slot] = tgt_all[:, slot * own:(slot + 1) * own]
    tpot_ref[...] = tgt_rows[slot_me]
    for d in range(1, n_tgt):
        t_from = (t_me + d) % n_tgt
        remote(
            mstat.at[t_from], mstat.at[t_from], ms.at[t_me], mr.at[t_from], s_me, t_from
        ).wait_recv()
    mass = mstat[0]
    for t in range(1, n_tgt):
        mass += mstat[t]
    for k in range(pieces):
        from_partner(x_me, k)
        keep[k] += recvp[x_me, k].astype(jnp.float32)
    for k in range(pieces):
        value = keep[k]
        for x in others:
            remote(
                sendx.at[x, k], recvx.at[x, k], xs.at[x, k], xr.at[x, k],
                s_me, x * 2 + c_me,
            ).wait_recv()
            value += recvx[x, k].astype(jnp.float32)
        value = value / mass[:, k * chunk:(k + 1) * chunk]
        out_ref[pl.ds(k * chunk, chunk), :] = value.T.astype(jnp.bfloat16)
    for copy in sent:
        copy.wait_send()


def finish(mapped_ref, spot_ref, tpot_ref, mapped_out, spot_out, tpot_out, sems):
    copies = [
        pltpu.make_async_copy(source, target, sems.at[i])
        for i, (source, target) in enumerate(
            ((mapped_ref, mapped_out), (spot_ref, spot_out), (tpot_ref, tpot_out))
        )
    ]
    for copy in copies:
        copy.start()
    for copy in copies:
        copy.wait()


def body(n_src, n_tgt, sources, log_src, targets, potential, log_tgt):
    rows, feats = sources.shape
    own = targets.shape[0]
    a_n, x_n = n_src // 2, n_tgt // 2
    group = n_src * own
    width = feats // n_tgt
    chunk = min(512, rows)
    pieces = rows // chunk
    f32, bf16 = jnp.float32, jnp.bfloat16
    dma = pltpu.SemaphoreType.DMA
    vmem = pl.BlockSpec(memory_space=pltpu.VMEM)
    hbm = pl.BlockSpec(memory_space=pltpu.HBM)
    padded = -(-own // LANES) * LANES
    spot, tpot, mapped = pl.pallas_call(
        functools.partial(kernel, n_src, n_tgt, chunk),
        name="sinkhorn",
        out_shape=(
            jax.ShapeDtypeStruct((1, rows), f32),
            jax.ShapeDtypeStruct((1, own), f32),
            jax.ShapeDtypeStruct((rows, width), bf16),
        ),
        in_specs=[hbm] * 5,
        out_specs=(vmem, vmem, vmem),
        scratch_shapes=[
            pltpu.VMEM((1, rows), f32),
            pltpu.VMEM((1, own), f32),
            pltpu.VMEM((1, own), f32),
            pltpu.VMEM((rows, feats), bf16),
            pltpu.VMEM((feats, rows), bf16),
            pltpu.VMEM((group, feats), bf16),
            pltpu.VMEM((feats, group), bf16),
            pltpu.VMEM((group, rows), f32),
            pltpu.VMEM((group, rows), bf16),
            pltpu.VMEM((n_src, 2, padded), f32),
            pltpu.VMEM((n_tgt, 1, rows), f32),
            pltpu.VMEM((n_src, 1, group), f32),
            pltpu.VMEM((n_tgt, 1, rows), f32),
            pltpu.VMEM((x_n, pieces, width, chunk), bf16),
            pltpu.VMEM((x_n, pieces, width, chunk), bf16),
            pltpu.VMEM((pieces, width, chunk), f32),
            pltpu.VMEM((x_n, pieces, width, chunk), bf16),
            pltpu.VMEM((x_n, pieces, width, chunk), bf16),
            pltpu.VMEM((1, group), f32),
            pltpu.VMEM((1, group), f32),
            pltpu.VMEM((n_src, 1, own), f32),
            dma((4,)),
            dma((a_n,)), dma((a_n,)), dma((a_n,)), dma((a_n,)),
            dma((n_src,)), dma((n_src,)),
            dma((n_tgt,)), dma((n_tgt,)),
            dma((n_src,)), dma((n_src,)),
            dma((n_tgt,)), dma((n_tgt,)),
            dma((x_n, pieces)), dma((x_n, pieces)),
            dma((x_n, pieces)), dma((x_n, pieces)),
        ],
        compiler_params=pltpu.CompilerParams(
            collective_id=0, has_side_effects=True, vmem_limit_bytes=40 * 1024 * 1024
        ),
    )(
        *(
            pltpu.with_memory_space_constraint(array, pltpu.HBM)
            for array in (
                sources, log_src.reshape(1, rows), targets,
                potential.reshape(1, own), log_tgt.reshape(1, own),
            )
        )
    )
    mapped, spot, tpot = pl.pallas_call(
        finish,
        name="finish",
        out_shape=(
            jax.ShapeDtypeStruct((rows, width), bf16),
            jax.ShapeDtypeStruct((1, rows), f32),
            jax.ShapeDtypeStruct((1, own), f32),
        ),
        in_specs=[pl.BlockSpec(memory_space=pl.ANY)] * 3,
        out_specs=(hbm,) * 3,
        scratch_shapes=[dma((3,))],
        compiler_params=pltpu.CompilerParams(vmem_limit_bytes=1024 * 1024),
    )(mapped, spot, tpot)
    return spot.reshape(rows), tpot.reshape(own), mapped


def solution(mesh):
    placed = (
        P("src", None),
        P("src"),
        P(("src", "tgt"), None),
        P(("src", "tgt")),
        P(("src", "tgt")),
    )
    return jax.shard_map(
        functools.partial(body, mesh.shape["src"], mesh.shape["tgt"]),
        mesh=mesh,
        in_specs=placed,
        out_specs=(P("src"), P(("src", "tgt")), P("src", "tgt")),
        check_vma=False,
    )
```
